256 devices in a mesh: feat: 16 (over z_lo, y), tok: 16 (over z_hi, x, core).
Axes of the slice: x: 4, y: 4, z: 8 (z_hi: 2, z_lo: 4; z = z_hi * 4 + z_lo), core: 2. Of those that a mesh axis runs over, the one named last changes fastest.
Arguments:
- tokens: bfloat16 [16384, 16384], P('tok', 'feat'), parts along dimension 0, may hold values from -6 to 6
- pair_weights: bfloat16 [2, 2048, 16384], P(None, None, 'feat'), may hold values from -0.125 to 0.125
- rank_down: bfloat16 [16384, 256], P('feat'), may hold values from -0.046875 to 0.046875
- rank_up: bfloat16 [256, 16384], P(None, 'feat'), may hold values from -0.375 to 0.375
Outputs:
- mixed: bfloat16 [16384, 16384], P('tok', 'feat'), parts along dimension 0
The draws below stay inside these ranges and needn't reach their ends.
There are 16 independent parts, one for each index of `tok`. The reference program is written for one: setup_inputs(seed, part) draws one part's arguments, and reference() takes and returns one part's arrays. A program takes and returns all parts, laid end to end along the dimension named above; an argument that names none is the same for every part. Nothing has to cross between parts.
All inputs are finite; a program needn't handle non-finite values.
Results may differ from the reference program's by a relative error of at most 0.0049.
Values may be sent and summed in bfloat16 or wider, within the bound.
No kernel may reach another device: no remote copies, remote signals or barrier semaphores. Data moves between devices by JAX's collectives and lax.ppermute only.
A program may use at most 64 MiB of HBM per device.

```python
import jax
import jax.numpy as jnp
import numpy as np

BLOCK = 1024
RANK = 256
SECTIONS = 2
TOK = 1024
D = 16384
N_FEAT = 16


def block_levels(stream_key, shape, shards, smallest, largest):
    def one(position, blocks):
        heights = jax.random.uniform(jax.random.fold_in(jax.random.fold_in(stream_key, 6), position), (blocks,), jnp.float32, smallest / len(shards), largest / len(shards))
        return jnp.repeat(jnp.exp(heights), shape[position] // blocks).reshape((-1,) + (1,) * (len(shape) - position - 1))

    gain = one(*shards[0])
    for cut in shards[1:]:
        gain = gain * one(*cut)
    return gain


def gaussian(stream_key, shape, spread, bound, cuts=(), kind=jnp.bfloat16):
    values = jax.random.normal(stream_key, shape, jnp.float32) * spread
    if len(cuts) > 0:
        values = block_levels(stream_key, shape, cuts, -0.22, 0.18) * values
    return jnp.clip(values, min=-bound, max=bound).astype(kind)


def setup_inputs(seed: int = 0, part: int = 0) -> dict:
    seeds = jax.random.split(jax.random.key(seed), 5)
    own_keys = jax.random.split(jax.random.fold_in(seeds[4], part), 5)
    return {
        "tokens": gaussian(own_keys[0], (TOK, D), 1.0, 6.0, ((1, 16),)),
        "pair_weights": gaussian(seeds[1], (SECTIONS, 2 * BLOCK, D), (2 * BLOCK) ** -0.5, 0.125, ((2, 16),)),
        "rank_down": gaussian(seeds[2], (D, RANK), D ** -0.5, 0.046875, ((0, 16),)),
        "rank_up": gaussian(seeds[3], (RANK, D), RANK ** -0.5, 0.375, ((1, 16),)),
    }


def section_apply(current, section_weight, bit_number):
    blocked = current.reshape(TOK, N_FEAT, BLOCK).astype(jnp.float32)
    order = np.arange(N_FEAT) ^ (1 << bit_number)
    partner_blocks = blocked[:, order, :]
    weight_blocks = section_weight.reshape(2 * BLOCK, N_FEAT, BLOCK).astype(jnp.float32)
    own_part = jnp.einsum("tkb,bkc->tkc", blocked, weight_blocks[:BLOCK])
    other_part = jnp.einsum("tkb,bkc->tkc", partner_blocks, weight_blocks[BLOCK:])
    return (own_part + other_part).reshape(TOK, N_FEAT * BLOCK)


def reference(tokens, pair_weights, rank_down, rank_up):
    bit_levels = N_FEAT.bit_length() - 1
    current = tokens
    activated = None
    for section_index in range(SECTIONS):
        bit_number = section_index * (bit_levels - 1) // (SECTIONS - 1)
        pre_act = section_apply(current, pair_weights[section_index], bit_number)
        activated = jax.nn.silu(pre_act)
        current = activated.astype(jnp.bfloat16)
    low_rank = jnp.dot(tokens, rank_down, preferred_element_type=jnp.float32).astype(jnp.bfloat16)
    branch_out = jnp.dot(low_rank, rank_up, preferred_element_type=jnp.float32)
    return (activated + branch_out).astype(jnp.bfloat16)
```

```python
import jax
import jax.numpy as jnp
from jax import lax
from jax.sharding import PartitionSpec as P

ROWS = (64, 128, 128, 128, 128, 128, 128, 128, 64)
BOUNDS = tuple((sum(ROWS[:i]), sum(ROWS[: i + 1])) for i in range(len(ROWS)))
LAST = len(ROWS) - 1
PIECES = 4


def exchanged(block, stride):
    count = lax.axis_size("feat")
    return lax.ppermute(block, "feat", [(i, i ^ stride) for i in range(count)])


def product(left, right):
    return jnp.dot(left, right, preferred_element_type=jnp.float32)


def halves(block, bit):
    half = block.shape[0] // 2
    kept = lax.dynamic_slice_in_dim(block, bit * half, half, 0)
    sent = lax.dynamic_slice_in_dim(block, (1 - bit) * half, half, 0)
    return kept, sent


def layer(tokens, pair_weights, rank_down, rank_up):
    width = tokens.shape[1]
    far = lax.axis_size("feat") // 2
    me = lax.axis_index("feat")
    b0, b1 = me & 1, (me >> 1) & 1
    mine = b1 * 2 + (b0 ^ b1)
    chunks = range(len(ROWS))

    w_own, w_other = pair_weights[0, :width], pair_weights[0, width:]
    n_own, n_other = pair_weights[1, :width], pair_weights[1, width:]

    def cut(source, k):
        return lax.slice_in_dim(source, *BOUNDS[k], axis=0)

    def after(done, k):
        source, done = lax.optimization_barrier((tokens, done))
        return cut(source, k), done

    rows, partner, own, state, received = [cut(tokens, 0)], [], [], [], []
    for k in chunks:
        if k == 1:
            chunk, own[0] = after(own[0], k)
            rows.append(chunk)
        elif k > 1:
            chunk, partner[k - 2] = after(partner[k - 2], k)
            rows.append(chunk)
        partner.append(exchanged(rows[k], 1))
        own.append(lax.optimization_barrier(product(rows[k], w_own)))
    for k in chunks:
        state.append(jax.nn.silu(own[k] + product(partner[k], w_other)).astype(jnp.bfloat16))
    for k in chunks:
        received.append(exchanged(state[k], far))

    kept, sent = halves(product(tokens, rank_down), b1)
    sent = sent.astype(jnp.bfloat16)
    for stride, bit in ((3, b0 ^ b1), (1, None)):
        got = exchanged(sent, stride)
        partial = kept + got.astype(jnp.float32)
        if bit is not None:
            kept, sent = halves(partial, bit)
    got = exchanged(partial, 4)
    partial = lax.optimization_barrier(partial + got)
    sent = partial.astype(jnp.bfloat16)
    got = exchanged(sent, far)
    low = (partial + got.astype(jnp.float32)).astype(jnp.bfloat16)
    got = exchanged(low, 1)
    low = jnp.concatenate([low, got], 0)
    got = exchanged(low, 3)
    low = jnp.concatenate([low, got], 0)
    piece = tokens.shape[0] // PIECES

    out = jnp.zeros(tokens.shape, jnp.bfloat16)
    for k, (a, b) in enumerate(BOUNDS):
        parts = []
        while a < b:
            block, offset = divmod(a, piece)
            size = min(b, (block + 1) * piece) - a
            parts.append(lax.dynamic_slice_in_dim(low, (block ^ mine) * piece + offset, size, 0))
            a += size
        side = product(jnp.concatenate(parts, 0), rank_up)
        side = lax.optimization_barrier(side)
        pre = lax.optimization_barrier(product(state[k], n_own))
        done = jax.nn.silu(pre + product(received[k], n_other))
        if k < LAST - 1:
            done = lax.optimization_barrier(done)
        out = lax.dynamic_update_slice_in_dim(out, (done + side).astype(jnp.bfloat16), BOUNDS[k][0], 0)
    return out


def solution(mesh):
    return jax.shard_map(
        layer,
        mesh=mesh,
        in_specs=(P("tok", "feat"), P(None, None, "feat"), P("feat", None), P(None, "feat")),
        out_specs=P("tok", "feat"),
        check_vma=False,
    )
```

```python
import jax
import jax.numpy as jnp
from jax import lax
from jax.experimental import pallas as pl
from jax.experimental.pallas import tpu as pltpu
from jax.sharding import PartitionSpec as P

ROWS = (64, 128, 128, 128, 128, 128, 128, 128, 64)
BOUNDS = tuple((sum(ROWS[:i]), sum(ROWS[: i + 1])) for i in range(len(ROWS)))
LAST = len(ROWS) - 1
PIECES = 8
OPENING = 2
FAST = 2


def exchanged(block, stride):
    count = lax.axis_size("feat")
    return lax.ppermute(block, "feat", [(i, i ^ stride) for i in range(count)])


def product(left, right):
    return jnp.dot(left, right, preferred_element_type=jnp.float32)


def opening(tokens, weights, sizes):
    width = tokens.shape[1]
    rows = sum(sizes)

    def body(t_ref, w_ref, *refs):
        *own_refs, other_ref, rows_ref, own_w_ref, sems = refs
        copies = [
            pltpu.make_async_copy(t_ref.at[pl.ds(0, rows)], rows_ref, sems.at[0]),
            pltpu.make_async_copy(w_ref.at[0, pl.ds(0, width)], own_w_ref, sems.at[1]),
            pltpu.make_async_copy(w_ref.at[0, pl.ds(width, width)], other_ref, sems.at[2]),
        ]
        for copy in copies:
            copy.start()
        copies[0].wait()
        copies[1].wait()
        start = 0
        for own_ref, size in zip(own_refs, sizes):
            own_ref[...] = product(rows_ref[pl.ds(start, size)], own_w_ref[...])
            start += size
        copies[2].wait()

    return pl.pallas_call(
        body,
        out_shape=(
            *(pltpu.VMEM((size, width), jnp.float32) for size in sizes),
            pltpu.VMEM((width, width), weights.dtype),
        ),
        in_specs=[pl.BlockSpec(memory_space=pl.ANY), pl.BlockSpec(memory_space=pl.ANY)],
        out_specs=tuple(pl.BlockSpec(memory_space=pltpu.VMEM) for _ in range(len(sizes) + 1)),
        scratch_shapes=[
            pltpu.VMEM((rows, width), tokens.dtype),
            pltpu.VMEM((width, width), weights.dtype),
            pltpu.SemaphoreType.DMA((3,)),
        ],
        compiler_params=pltpu.CompilerParams(vmem_limit_bytes=56 << 20),
        name="opening",
    )(tokens, weights)


def halves(block, bit):
    half = block.shape[0] // 2
    kept = lax.dynamic_slice_in_dim(block, bit * half, half, 0)
    sent = lax.dynamic_slice_in_dim(block, (1 - bit) * half, half, 0)
    return kept, sent


def layer(tokens, pair_weights, rank_down, rank_up):
    width = tokens.shape[1]
    far = lax.axis_size("feat") // 2
    me = lax.axis_index("feat")
    b0, b1, b2 = me & 1, (me >> 1) & 1, (me >> 2) & 1
    mine = (b1 * 2 + (b0 ^ b1)) * 2 + b2
    chunks = range(len(ROWS))

    w_own, w_other = pair_weights[0, :width], pair_weights[0, width:]
    n_own, n_other = pair_weights[1, :width], pair_weights[1, width:]

    def cut(source, k):
        return lax.slice_in_dim(source, *BOUNDS[k], axis=0)

    def after(done, k):
        source, done = lax.optimization_barrier((tokens, done))
        return cut(source, k), done

    rows, partner, own, state, received = [cut(tokens, 0)], [], [], [], []
    for k in chunks:
        if k == 1:
            chunk, rank_up = after(rank_up, k)
            rows.append(chunk)
        elif k > 1:
            chunk, partner[k - 2] = after(partner[k - 2], k)
            rows.append(chunk)
        partner.append(exchanged(rows[k], 1))
        if k == 0:
            *own, fast_other = opening(tokens, pair_weights, ROWS[:OPENING])
        elif k >= OPENING:
            own.append(lax.optimization_barrier(product(rows[k], w_own)))
    for k in chunks:
        left = fast_other if k < FAST else w_other
        state.append(jax.nn.silu(own[k] + product(partner[k], left)).astype(jnp.bfloat16))
    for k in chunks:
        received.append(exchanged(state[k], far))

    kept, sent = halves(product(tokens, rank_down), b1)
    sent = sent.astype(jnp.bfloat16)
    for stride, bit in ((3, b0 ^ b1), (1, b2)):
        got = exchanged(sent, stride)
        partial = kept + got.astype(jnp.float32)
        kept, sent = halves(partial, bit)
    got = exchanged(sent, 4)
    partial = lax.optimization_barrier(kept + got)
    sent = partial.astype(jnp.bfloat16)
    got = exchanged(sent, far)
    low = (partial + got.astype(jnp.float32)).astype(jnp.bfloat16)
    got = exchanged(low, 4)
    low = jnp.concatenate([low, got], 0)
    got = exchanged(low, 1)
    low = jnp.concatenate([low, got], 0)
    got = exchanged(low, 3)
    low = jnp.concatenate([low, got], 0)
    piece = tokens.shape[0] // PIECES

    out = jnp.zeros(tokens.shape, jnp.bfloat16)
    for k, (a, b) in enumerate(BOUNDS):
        parts = []
        while a < b:
            block, offset = divmod(a, piece)
            size = min(b, (block + 1) * piece) - a
            parts.append(lax.dynamic_slice_in_dim(low, (block ^ mine) * piece + offset, size, 0))
            a += size
        side = product(jnp.concatenate(parts, 0), rank_up)
        side = lax.optimization_barrier(side)
        pre = lax.optimization_barrier(product(state[k], n_own))
        done = jax.nn.silu(pre + product(received[k], n_other))
        if k < LAST - 1:
            done = lax.optimization_barrier(done)
        out = lax.dynamic_update_slice_in_dim(out, (done + side).astype(jnp.bfloat16), BOUNDS[k][0], 0)
    return out


def solution(mesh):
    return jax.shard_map(
        layer,
        mesh=mesh,
        in_specs=(P("tok", "feat"), P(None, None, "feat"), P("feat", None), P(None, "feat")),
        out_specs=P("tok", "feat"),
        check_vma=False,
    )
```

```python
import jax
import jax.numpy as jnp
from jax import lax
from jax.experimental import pallas as pl
from jax.experimental.pallas import tpu as pltpu
from jax.sharding import PartitionSpec as P

ROWS = (64, 64, 128, 128, 128, 128, 160, 160, 64)
BOUNDS = tuple((sum(ROWS[:i]), sum(ROWS[: i + 1])) for i in range(len(ROWS)))
LAST = len(ROWS) - 1
PIECES = 8
OPENING = 2
PARTS = 4
LIMIT = 54
FAST = 2


def exchanged(block, stride):
    count = lax.axis_size("feat")
    return lax.ppermute(block, "feat", [(i, i ^ stride) for i in range(count)])


def product(left, right):
    return jnp.dot(left, right, preferred_element_type=jnp.float32)


def opening(tokens, weights, sizes):
    width = tokens.shape[1]
    count = len(sizes)
    piece = width // PARTS

    def body(t_ref, w_ref, *refs):
        own_refs, chunk_refs = refs[:count], refs[count : 2 * count - 1]
        other_ref, first_ref, own_w_ref, sems = refs[2 * count - 1 :]
        chunk_refs = (first_ref, *chunk_refs)
        loads = []
        start = 0
        for ref, size in zip(chunk_refs, sizes):
            loads.append((t_ref.at[pl.ds(start, size)], ref))
            start += size
        for offset, ref in ((0, own_w_ref), (width, other_ref)):
            for k in range(PARTS):
                loads.append(
                    (w_ref.at[0, pl.ds(offset + k * piece, piece)], ref.at[pl.ds(k * piece, piece)])
                )
        copies = [pltpu.make_async_copy(*load, sems.at[i]) for i, load in enumerate(loads)]
        for copy in copies:
            copy.start()
        for copy in copies[: count + PARTS]:
            copy.wait()
        for own_ref, ref in zip(own_refs, chunk_refs):
            own_ref[...] = product(ref[...], own_w_ref[...])
        for copy in copies[count + PARTS :]:
            copy.wait()

    return pl.pallas_call(
        body,
        out_shape=(
            *(pltpu.VMEM((size, width), jnp.float32) for size in sizes),
            *(pltpu.VMEM((size, width), tokens.dtype) for size in sizes[1:]),
            pltpu.VMEM((width, width), weights.dtype),
        ),
        in_specs=[pl.BlockSpec(memory_space=pl.ANY), pl.BlockSpec(memory_space=pl.ANY)],
        out_specs=tuple(pl.BlockSpec(memory_space=pltpu.VMEM) for _ in range(2 * count)),
        scratch_shapes=[
            pltpu.VMEM((sizes[0], width), tokens.dtype),
            pltpu.VMEM((width, width), weights.dtype),
            pltpu.SemaphoreType.DMA((count + 2 * PARTS,)),
        ],
        compiler_params=pltpu.CompilerParams(vmem_limit_bytes=LIMIT << 20),
        name="opening",
    )(tokens, weights)


def halves(block, bit):
    half = block.shape[0] // 2
    kept = lax.dynamic_slice_in_dim(block, bit * half, half, 0)
    sent = lax.dynamic_slice_in_dim(block, (1 - bit) * half, half, 0)
    return kept, sent


def layer(tokens, pair_weights, rank_down, rank_up):
    width = tokens.shape[1]
    far = lax.axis_size("feat") // 2
    me = lax.axis_index("feat")
    b0, b1, b2 = me & 1, (me >> 1) & 1, (me >> 2) & 1
    mine = (b1 * 2 + (b0 ^ b1)) * 2 + b2
    chunks = range(len(ROWS))

    w_own, w_other = pair_weights[0, :width], pair_weights[0, width:]
    n_own, n_other = pair_weights[1, :width], pair_weights[1, width:]

    def cut(source, k):
        return lax.slice_in_dim(source, *BOUNDS[k], axis=0)

    def after(done, k):
        source, done = lax.optimization_barrier((tokens, done))
        return cut(source, k), done

    rows, partner, state, received = [cut(tokens, 0)], [], [], []
    made = opening(tokens, pair_weights, ROWS[:OPENING])
    own = list(made[:OPENING])
    rows += made[OPENING:-1]
    fast_other = made[-1]
    for k in chunks:
        if k >= OPENING:
            chunk, partner[k - 2] = after(partner[k - 2], k)
            rows.append(chunk)
        partner.append(exchanged(rows[k], 1))
        if k >= OPENING:
            own.append(lax.optimization_barrier(product(rows[k], w_own)))
    for k in chunks:
        left = fast_other if k < FAST else w_other
        state.append(jax.nn.silu(own[k] + product(partner[k], left)).astype(jnp.bfloat16))
    for k in chunks:
        received.append(exchanged(state[k], far))

    kept, sent = halves(product(tokens, rank_down), b1)
    sent = sent.astype(jnp.bfloat16)
    for stride, bit in ((3, b0 ^ b1), (1, b2)):
        got = exchanged(sent, stride)
        partial = kept + got.astype(jnp.float32)
        kept, sent = halves(partial, bit)
    got = exchanged(sent, 4)
    partial = lax.optimization_barrier(kept + got)
    sent = partial.astype(jnp.bfloat16)
    got = exchanged(sent, far)
    low = (partial + got.astype(jnp.float32)).astype(jnp.bfloat16)
    got = exchanged(low, 4)
    low = jnp.concatenate([low, got], 0)
    got = exchanged(low, 1)
    low = jnp.concatenate([low, got], 0)
    got = exchanged(low, 3)
    low = jnp.concatenate([low, got], 0)
    piece = tokens.shape[0] // PIECES

    out = jnp.zeros(tokens.shape, jnp.bfloat16)
    for k, (a, b) in enumerate(BOUNDS):
        parts = []
        while a < b:
            block, offset = divmod(a, piece)
            size = min(b, (block + 1) * piece) - a
            parts.append(lax.dynamic_slice_in_dim(low, (block ^ mine) * piece + offset, size, 0))
            a += size
        side = product(jnp.concatenate(parts, 0), rank_up)
        side = lax.optimization_barrier(side)
        pre = lax.optimization_barrier(product(state[k], n_own))
        done = jax.nn.silu(pre + product(received[k], n_other))
        if k < LAST - 1:
            done = lax.optimization_barrier(done)
        out = lax.dynamic_update_slice_in_dim(out, (done + side).astype(jnp.bfloat16), BOUNDS[k][0], 0)
    return out


def solution(mesh):
    return jax.shard_map(
        layer,
        mesh=mesh,
        in_specs=(P("tok", "feat"), P(None, None, "feat"), P("feat", None), P(None, "feat")),
        out_specs=P("tok", "feat"),
        check_vma=False,
    )
```
